512 devices in a mesh: layer: 32 (over z_lo, x, core), dp: 8 (over y), mp: 2 (over z_hi).
Axes of the slice: x: 4, y: 8, z: 8 (z_hi: 2, z_lo: 4; z = z_hi * 4 + z_lo), core: 2. Of those that a mesh axis runs over, the one named last changes fastest.
Arguments:
- states: bfloat16 [128, 1024, 1024], P('layer', 'dp'), may hold values from -6 to 6
- weights: bfloat16 [128, 1024, 1024], P('layer', 'dp', 'mp'), may hold values from -0.1875 to 0.1875
- guess_points: bfloat16 [32, 1024, 1024], P('layer', 'dp'), may hold values from -2 to 2
- cotangent: bfloat16 [1024, 1024], P('dp'), may hold values from -6 to 6
Outputs:
- adjoint: bfloat16 [128, 1024, 1024], P('layer', 'dp', 'mp')
- weight_grads: float32 [128, 1024, 1024], P('layer', 'dp', 'mp')
The draws below stay inside these ranges and needn't reach their ends.
All inputs are finite; a program needn't handle non-finite values.
Results may differ from the reference program's by a relative error of at most 0.03.
Values may be sent and summed in bfloat16 or wider, within the bound.
No kernel may reach another device: no remote copies, remote signals or barrier semaphores. Data moves between devices by JAX's collectives and lax.ppermute only.
A program may use at most 64 MiB of HBM per device.

```python
import jax
import jax.numpy as jnp
from jax import lax

D = 1024
ROWS_DEV = 128
LAYERS = 128
COARSE = 32
ROWS = 1024


def level_of(own_key, shape, shards, least, top_value):
    loudness, own = 1.0, jax.random.fold_in(own_key, 6)
    for dim, parts in shards:
        draws = jnp.exp(jax.random.uniform(jax.random.fold_in(own, dim), (parts,), jnp.float32, least / len(shards), top_value / len(shards)))
        loudness = loudness * jnp.repeat(draws, shape[dim] // parts).reshape([-1 if axis == dim else 1 for axis in range(len(shape))])
    return loudness


def scatter_about(stream_key, extent, deviation, most, split=(), dtype=jnp.bfloat16):
    entries = deviation * jax.random.normal(stream_key, extent, jnp.float32)
    if split:
        entries = entries * level_of(stream_key, extent, split, -0.22, 0.18)
    return jnp.clip(entries, -most, most).astype(dtype)


def setup_inputs(seed: int = 0) -> dict:
    arg_keys = jax.random.split(jax.random.key(seed), 5)
    return {
        "states": scatter_about(arg_keys[0], (LAYERS, ROWS, D), 1.0, 6.0, ((0, 32), (1, 8))),
        "weights": scatter_about(arg_keys[1], (LAYERS, D, D), D ** -0.5, 0.1875, ((0, 32), (1, 8), (2, 2))),
        "guess_points": scatter_about(arg_keys[2], (COARSE, ROWS, D), 0.3, 2.0, ((0, 32), (1, 8))),
        "cotangent": scatter_about(arg_keys[3], (ROWS, D), 1.0, 6.0, ((0, 8),)),
    }


step_size = 0.1


def slope_of(inputs, weight_block):
    tangent = jnp.tanh(jnp.dot(inputs, weight_block, preferred_element_type=jnp.float32))
    return 1.0 - tangent * tangent


def apply_step(upper_adj, slope, weight_block, coefficient):
    scaled_rows = (upper_adj * slope).astype(jnp.bfloat16)
    product = jnp.dot(scaled_rows, weight_block.T, preferred_element_type=jnp.float32)
    return upper_adj + coefficient * product, scaled_rows


def reference(states, weights, guess_points, cotangent):
    layer_total = states.shape[0]
    point_total = guess_points.shape[0]
    factor = layer_total // point_total
    model_width = states.shape[2]
    terminal = cotangent.astype(jnp.float32)
    slopes = [None] * layer_total
    residuals = [None] * point_total
    upper_adj = terminal
    for layer_id in range(layer_total - 1, -1, -1):
        slopes[layer_id] = slope_of(states[layer_id], weights[layer_id])
        relaxed, unused = apply_step(upper_adj, slopes[layer_id], weights[layer_id], step_size)
        if layer_id % factor == 0:
            base_point = guess_points[layer_id // factor].astype(jnp.float32)
            residuals[layer_id // factor] = relaxed - base_point
            upper_adj = base_point
        else:
            upper_adj = relaxed
    errors = [None] * point_total
    carried = jnp.zeros_like(terminal)
    for point_id in range(point_total - 1, -1, -1):
        layer_id = point_id * factor
        stepped, unused = apply_step(carried, slopes[layer_id], weights[layer_id], factor * step_size)
        errors[point_id] = (stepped + residuals[point_id]).astype(jnp.bfloat16)
        carried = lax.optimization_barrier(errors[point_id]).astype(jnp.float32)
    adjoints = [None] * layer_total
    gradients = [None] * layer_total
    block_count = states.shape[1] // ROWS_DEV
    upper_adj = terminal
    for layer_id in range(layer_total - 1, -1, -1):
        current, scaled_rows = apply_step(upper_adj, slopes[layer_id], weights[layer_id], step_size)
        if layer_id % factor == 0:
            point_id = layer_id // factor
            current = guess_points[point_id].astype(jnp.float32) + errors[point_id].astype(jnp.float32)
        blocks_in = states[layer_id].reshape(block_count, ROWS_DEV, model_width).astype(jnp.float32)
        blocks_scaled = scaled_rows.reshape(block_count, ROWS_DEV, model_width).astype(jnp.float32)
        partial_terms = jnp.einsum("brd,brh->bdh", blocks_in, blocks_scaled).astype(jnp.bfloat16)
        partial_terms = lax.optimization_barrier(partial_terms).astype(jnp.float32)
        gradients[layer_id] = step_size * jnp.sum(partial_terms, axis=0)
        adjoints[layer_id] = current.astype(jnp.bfloat16)
        upper_adj = current
    return jnp.stack(adjoints), jnp.stack(gradients)
```

```python
import functools

import jax
import jax.numpy as jnp
from jax import lax
from jax.experimental import pallas as pl
from jax.experimental.pallas import tpu as pltpu
from jax.sharding import Mesh
from jax.sharding import PartitionSpec as P

step_size = 0.1
BF = jnp.bfloat16
F32 = jnp.float32
LAYER = ("zl", "x", "core")
RING = ("x", "core")


def back_product(scaled, weight):
    return lax.dot_general(scaled, weight, (((1,), (1,)), ((), ())), preferred_element_type=F32)


def swapped(value, axis):
    return lax.ppermute(value, axis, [(0, 1), (1, 0)])


def rotated(value, axis, steps):
    count = lax.axis_size(axis)
    return lax.ppermute(value, axis, [(i, (i + steps) % count) for i in range(count)])


def relax_kernel(blocks, states_ref, rest_ref, coarse_ref, term_ref, guess_ref, slopes_ref, pack_ref, v_ref):
    turn = pl.program_id(0)
    last = pl.num_programs(0) - 1
    rows, width = v_ref.shape

    @pl.when(turn == 0)
    def _():
        v_ref[...] = term_ref[...].astype(F32)

    def step(weight):
        tangent = jnp.tanh(jnp.dot(states_ref[0], weight, preferred_element_type=F32))
        slope = 1.0 - tangent * tangent
        slopes_ref[0] = slope
        scaled = (v_ref[...] * slope).astype(BF)
        return v_ref[...] + step_size * back_product(scaled, weight), slope

    @pl.when(turn < last)
    def _():
        v_ref[...] = step(rest_ref[0])[0]

    @pl.when(turn == last)
    def _():
        relaxed, slope = step(coarse_ref[...])
        residual = relaxed - guess_ref[...].astype(F32)
        part = rows // blocks
        pack_ref[:, :part, :] = residual.astype(BF).reshape(blocks, part, width)
        pack_ref[:, part:, :] = slope.astype(BF).reshape(blocks, part, width)


def relax(states, rest, coarse, terminal, guess, blocks):
    layers, rows, width = states.shape
    top = layers - 1
    return pl.pallas_call(
        functools.partial(relax_kernel, blocks),
        grid=(layers,),
        in_specs=[
            pl.BlockSpec((1, rows, width), lambda t: (top - t, 0, 0)),
            pl.BlockSpec((1, width, width), lambda t: (jnp.maximum(top - 1 - t, 0), 0, 0)),
            pl.BlockSpec((width, width), lambda t: (0, 0)),
            pl.BlockSpec((rows, width), lambda t: (0, 0)),
            pl.BlockSpec((rows, width), lambda t: (0, 0)),
        ],
        out_specs=[
            pl.BlockSpec((1, rows, width), lambda t: (top - t, 0, 0)),
            pl.BlockSpec((blocks, 2 * rows // blocks, width), lambda t: (0, 0, 0)),
        ],
        out_shape=[
            jax.ShapeDtypeStruct((layers, rows, width), F32),
            jax.ShapeDtypeStruct((blocks, 2 * rows // blocks, width), BF),
        ],
        scratch_shapes=[pltpu.VMEM((rows, width), F32)],
        compiler_params=pltpu.CompilerParams(vmem_limit_bytes=40 * 2**20),
        name="relax",
    )(states, rest, coarse, terminal, guess)


def chain_kernel(count, place_ref, pack_ref, own_ref, other_ref, in_ref, out_ref, low_ref, v_ref):
    turn = pl.program_id(0)
    part = in_ref.shape[0]
    scale = 4 * step_size
    chip = count - 1 - turn

    @pl.when(turn == 0)
    def _():
        v_ref[...] = in_ref[...].astype(F32)

    def two(high, low):
        v = v_ref[...]
        for side, weight in ((1, high), (0, low)):
            point = 2 * chip + side
            scaled = (v * pack_ref[point, part:, :].astype(F32)).astype(BF)
            out_ref[point, :part, :] = v.astype(BF)
            residual = pack_ref[point, :part, :].astype(F32)
            short = (v + scale * back_product(scaled, weight[0]) + residual).astype(BF)
            out_ref[point, part:, :] = short
            v = short.astype(F32)
        v_ref[...] = v
        low_ref[...] = v.astype(BF)

    @pl.when(place_ref[1] == 1)
    def _():
        two(own_ref, other_ref)

    @pl.when(place_ref[1] == 0)
    def _():
        two(other_ref, own_ref)


def chain(place, pack, own, other, incoming):
    count, width = own.shape[0], own.shape[1]
    part = incoming.shape[0]
    weight_spec = pl.BlockSpec((1, width, width), lambda t, place: ((2 * count - 1 - t - place[0]) % count, 0, 0))
    return pl.pallas_call(
        functools.partial(chain_kernel, count),
        grid_spec=pltpu.PrefetchScalarGridSpec(
            num_scalar_prefetch=1,
            grid=(count,),
            in_specs=[
                pl.BlockSpec((2 * count, 2 * part, width), lambda t, place: (0, 0, 0)),
                weight_spec,
                weight_spec,
                pl.BlockSpec((part, width), lambda t, place: (0, 0)),
            ],
            out_specs=[
                pl.BlockSpec((2 * count, 2 * part, width), lambda t, place: (0, 0, 0)),
                pl.BlockSpec((part, width), lambda t, place: (0, 0)),
            ],
            scratch_shapes=[pltpu.VMEM((part, width), F32)],
        ),
        out_shape=[
            jax.ShapeDtypeStruct((2 * count, 2 * part, width), BF),
            jax.ShapeDtypeStruct((part, width), BF),
        ],
        compiler_params=pltpu.CompilerParams(vmem_limit_bytes=40 * 2**20),
        name="chain",
    )(place, pack, own, other, incoming)


def correct_kernel(place_ref, spread_ref, states_ref, slopes_ref, rest_ref, term_ref, guess_ref, adj_ref, part_ref, v_ref):
    turn = pl.program_id(0)
    last = pl.num_programs(0) - 1
    rows, width = v_ref.shape
    half = width // 2
    part = spread_ref.shape[1] // 2

    def own_half(value):
        return jnp.where(place_ref[2] == 0, value[:, :half], value[:, half:])

    @pl.when(turn == 0)
    def _():
        error = spread_ref[:, :part, :].reshape(rows, width)
        v_ref[...] = term_ref[...].astype(F32) + error.astype(F32)

    scaled = (v_ref[...] * slopes_ref[0]).astype(BF)
    terms = lax.dot_general(
        states_ref[0], own_half(scaled), (((0,), (0,)), ((), ())), preferred_element_type=F32
    )
    part_ref[0] = terms.astype(BF)

    @pl.when(turn < last)
    def _():
        current = v_ref[...] + step_size * back_product(scaled, rest_ref[0])
        v_ref[...] = current
        adj_ref[0] = own_half(current).astype(BF)

    @pl.when(turn == last)
    def _():
        error = spread_ref[:, part:, :].reshape(rows, width)
        adj_ref[0] = own_half(guess_ref[...].astype(F32) + error.astype(F32)).astype(BF)


def correct(place, spread, states, slopes, rest, terminal, guess):
    layers, rows, width = states.shape
    half = width // 2
    top = layers - 1
    return pl.pallas_call(
        correct_kernel,
        grid_spec=pltpu.PrefetchScalarGridSpec(
            num_scalar_prefetch=1,
            grid=(layers,),
            in_specs=[
                pl.BlockSpec(spread.shape, lambda t, place: (0, 0, 0)),
                pl.BlockSpec((1, rows, width), lambda t, place: (top - t, 0, 0)),
                pl.BlockSpec((1, rows, width), lambda t, place: (top - t, 0, 0)),
                pl.BlockSpec((1, width, width), lambda t, place: (jnp.maximum(top - 1 - t, 0), 0, 0)),
                pl.BlockSpec((rows, width), lambda t, place: (0, 0)),
                pl.BlockSpec((rows, width), lambda t, place: (0, 0)),
            ],
            out_specs=[
                pl.BlockSpec((1, rows, half), lambda t, place: (top - t, 0, 0)),
                pl.BlockSpec((1, width, half), lambda t, place: (top - t, 0, 0)),
            ],
            scratch_shapes=[pltpu.VMEM((rows, width), F32)],
        ),
        out_shape=[
            jax.ShapeDtypeStruct((layers, rows, half), BF),
            jax.ShapeDtypeStruct((layers, width, half), BF),
        ],
        compiler_params=pltpu.CompilerParams(vmem_limit_bytes=40 * 2**20),
        name="correct",
    )(place, spread, states, slopes, rest, terminal, guess)


def body(states, weights, guess_points, cotangent):
    slabs = lax.axis_size(LAYER)
    slab = lax.axis_index(LAYER)
    half_index = lax.axis_index("mp")
    place = jnp.stack([lax.axis_index("x"), lax.axis_index("core"), half_index]).astype(jnp.int32)
    blocks = lax.axis_size(RING)
    width = states.shape[2]
    mid = width // 2
    guess = guess_points[0]

    def whole_rows(own):
        other = swapped(own, "mp")
        return jnp.where(
            half_index == 0,
            jnp.concatenate([own, other], -1),
            jnp.concatenate([other, own], -1),
        )

    next_guess = lax.ppermute(guess, LAYER, [(i, i - 1) for i in range(1, slabs)])
    terminal = jnp.where(slab == slabs - 1, cotangent, next_guess)
    coarse = lax.all_gather(whole_rows(weights[0]), "dp", axis=0, tiled=True)
    rest = lax.all_gather(whole_rows(weights[1:]), "dp", axis=1, tiled=True)

    ahead = rotated(coarse, "x", -1)
    behind = rotated(coarse, "x", 1)
    across = jnp.concatenate([rotated(ahead[:mid], "x", -1), rotated(behind[mid:], "x", 1)], 0)
    own = jnp.stack([coarse, ahead, across, behind])
    other = swapped(own, "core")

    slopes, pack = relax(states, rest, coarse, terminal, guess, blocks)
    pack = lax.all_to_all(pack, RING, 0, 0, tiled=True)

    incoming = jnp.zeros((pack.shape[1] // 2, width), BF)
    stages = lax.axis_size("zl")
    for stage in range(stages):
        errors, lowest = chain(place, pack, own, other, incoming)
        if stage < stages - 1:
            incoming = lax.ppermute(lowest, "zl", [(i, i - 1) for i in range(1, stages)])
    spread = lax.all_to_all(errors, RING, 0, 0, tiled=True)

    adjoint, partial = correct(place, spread, states, slopes, rest, terminal, guess)
    grads = lax.psum_scatter(partial, "dp", scatter_dimension=1, tiled=True)
    return adjoint, step_size * grads.astype(F32)


def solution(mesh):
    slabs, rows, halves = (mesh.shape[name] for name in ("layer", "dp", "mp"))
    fine = Mesh(
        mesh.devices.reshape(slabs // 8, 4, 2, rows, halves), ("zl", "x", "core", "dp", "mp")
    )
    return jax.shard_map(
        body,
        mesh=fine,
        in_specs=(
            P(LAYER, "dp", None),
            P(LAYER, "dp", "mp"),
            P(LAYER, "dp", None),
            P("dp", None),
        ),
        out_specs=(P(LAYER, "dp", "mp"), P(LAYER, "dp", "mp")),
        check_vma=False,
    )
```

```python
import functools

import jax
import jax.numpy as jnp
from jax import lax
from jax.experimental import pallas as pl
from jax.experimental.pallas import tpu as pltpu
from jax.sharding import Mesh
from jax.sharding import PartitionSpec as P

step_size = 0.1
BF = jnp.bfloat16
F32 = jnp.float32
LAYER = ("zl", "x", "core")
RING = ("x", "core")


def back_product(scaled, weight):
    return lax.dot_general(scaled, weight, (((1,), (1,)), ((), ())), preferred_element_type=F32)


def swapped(value, axis):
    return lax.ppermute(value, axis, [(0, 1), (1, 0)])


def rotated(value, axis, steps):
    count = lax.axis_size(axis)
    return lax.ppermute(value, axis, [(i, (i + steps) % count) for i in range(count)])


def halves(value, index):
    half = value.shape[1] // 2
    low, high = value[:, :half], value[:, half:]
    return jnp.where(index == 0, low, high), jnp.where(index == 0, high, low)


def params(mib):
    return pltpu.CompilerParams(vmem_limit_bytes=mib * 2**20)


def cost(flops, moved):
    return pl.CostEstimate(flops=flops, bytes_accessed=moved, transcendentals=0)


def slope_kernel(states_ref, weight_ref, out_ref):
    tangent = jnp.tanh(jnp.dot(states_ref[0], weight_ref[0], preferred_element_type=F32))
    out_ref[0] = 1.0 - tangent * tangent


def slopes_of(states, weights, first):
    rows, width = states.shape[1:]
    layers, _, columns = weights.shape
    return pl.pallas_call(
        slope_kernel,
        grid=(layers,),
        in_specs=[
            pl.BlockSpec((1, rows, width), lambda t: (first + t, 0, 0)),
            pl.BlockSpec((1, width, columns), lambda t: (t, 0, 0)),
        ],
        out_specs=pl.BlockSpec((1, rows, columns), lambda t: (t, 0, 0)),
        out_shape=jax.ShapeDtypeStruct((layers, rows, columns), F32),
        compiler_params=params(56),
        cost_estimate=cost(2 * layers * rows * width * columns, 2 * layers * width * columns),
        name="slopes",
    )(states, weights)


def first_kernel(place_ref, term_ref, states_ref, weight_ref, keep_ref, send_ref):
    weight = weight_ref[0]
    tangent = jnp.tanh(jnp.dot(states_ref[0], weight, preferred_element_type=F32))
    upper = halves(term_ref[...], place_ref[2])[0].astype(F32)
    scaled = (upper * (1.0 - tangent * tangent)).astype(BF)
    own, other = halves(step_size * back_product(scaled, weight), place_ref[2])
    keep_ref[...] = upper + own
    send_ref[...] = other.astype(BF)


def middle_kernel(full, place_ref, kept_ref, got_ref, slope_ref, weight_ref, keep_ref, send_ref):
    upper = kept_ref[...] + got_ref[...].astype(F32)
    scaled = (upper * slope_ref[0]).astype(BF)
    product = step_size * back_product(scaled, weight_ref[0])
    if full:
        none = jnp.zeros_like(upper)
        first = place_ref[2] == 0
        sides = [jnp.where(first, upper, none), jnp.where(first, none, upper)]
        mine = product + jnp.concatenate(sides, 1)
        keep_ref[...] = mine
        send_ref[...] = mine.astype(BF)
    else:
        own, other = halves(product, place_ref[2])
        keep_ref[...] = upper + own
        send_ref[...] = other.astype(BF)


def half_step(place, operands, states, slopes, weights, layer, full=False):
    rows, width = states.shape[1:]
    columns = width if full else width // 2
    flat = [pl.BlockSpec(v.shape, lambda t, place: (0, 0)) for v in operands]
    pick = lambda v, i: pl.BlockSpec((1,) + v.shape[1:], lambda t, place: (i, 0, 0))
    if slopes is None:
        kernel, source, index = first_kernel, states, layer
    else:
        kernel, source, index = functools.partial(middle_kernel, full), slopes, layer - 1
    return pl.pallas_call(
        kernel,
        grid_spec=pltpu.PrefetchScalarGridSpec(
            num_scalar_prefetch=1,
            grid=(1,),
            in_specs=flat + [pick(source, index), pick(weights, layer - 1)],
            out_specs=[pl.BlockSpec((rows, columns), lambda t, place: (0, 0))] * 2,
        ),
        out_shape=[
            jax.ShapeDtypeStruct((rows, columns), F32),
            jax.ShapeDtypeStruct((rows, columns), BF),
        ],
        compiler_params=params(56 if slopes is None else 12),
        cost_estimate=cost(rows * width * width, width * width),
        name="half_step",
    )(place, *operands, source, weights)


def last_kernel(blocks, kept_ref, got_ref, slope_ref, weight_ref, guess_ref, pack_ref):
    rows, width = kept_ref.shape
    part = rows // blocks
    upper = kept_ref[...] + got_ref[...].astype(F32)
    slope = slope_ref[0]
    scaled = (upper * slope).astype(BF)
    relaxed = upper + step_size * back_product(scaled, weight_ref[...])
    residual = relaxed - guess_ref[...].astype(F32)
    pack_ref[:, :part, :] = residual.astype(BF).reshape(blocks, part, width)
    pack_ref[:, part:, :] = slope.astype(BF).reshape(blocks, part, width)


def last_step(kept, got, slope, weight, guess, blocks):
    rows, width = kept.shape
    return pl.pallas_call(
        functools.partial(last_kernel, blocks),
        out_shape=jax.ShapeDtypeStruct((blocks, 2 * rows // blocks, width), BF),
        compiler_params=params(16),
        cost_estimate=cost(2 * rows * width * width, 2 * width * width),
        name="last_step",
    )(kept, got, slope, weight, guess)


def chain_kernel(place_ref, pack_ref, in_ref, *rest):
    chips = (len(rest) - 4) // 2
    sources, (out_ref, low_ref, held, arrived) = rest[: 2 * chips], rest[2 * chips :]
    count = 2 * chips
    part = in_ref.shape[0]
    scale = 4 * step_size

    def fetch(source, point):
        return pltpu.make_async_copy(source, held.at[point], arrived.at[point])

    for point in range(count - 1, -1, -1):
        hop = lax.rem(point // 2 - place_ref[0] + chips, chips)
        same = place_ref[1] == point % 2
        for number in range(chips):
            @pl.when((hop == number) & same)
            def _():
                fetch(sources[number], point).start()

            @pl.when((hop == number) & jnp.logical_not(same))
            def _():
                fetch(sources[chips + number], point).start()

    short = in_ref[...]
    for point in range(count - 1, -1, -1):
        v = short.astype(F32)
        scaled = (v * pack_ref[point, part:, :].astype(F32)).astype(BF)
        out_ref[point, :part, :] = short
        residual = pack_ref[point, :part, :].astype(F32)
        fetch(sources[0], point).wait()
        short = (v + scale * back_product(scaled, held[point]) + residual).astype(BF)
        out_ref[point, part:, :] = short
    low_ref[...] = short


def chain(place, pack, sources, incoming):
    count = len(sources)
    weight = sources[0].shape
    whole = lambda v: pl.BlockSpec(v.shape, lambda t, place: (0,) * v.ndim)
    return pl.pallas_call(
        chain_kernel,
        grid_spec=pltpu.PrefetchScalarGridSpec(
            num_scalar_prefetch=1,
            grid=(1,),
            in_specs=[whole(pack), whole(incoming)] + [pl.BlockSpec(memory_space=pl.ANY)] * count,
            out_specs=[whole(pack), whole(incoming)],
            scratch_shapes=[
                pltpu.VMEM((count,) + weight, BF),
                pltpu.SemaphoreType.DMA((count,)),
            ],
        ),
        out_shape=[
            jax.ShapeDtypeStruct(pack.shape, BF),
            jax.ShapeDtypeStruct(incoming.shape, BF),
        ],
        compiler_params=params(40),
        cost_estimate=cost(2 * pack.size * weight[0], 2 * count * weight[0] * weight[1]),
        name="chain",
    )(place, pack, incoming, *sources)


def correct_kernel(
    place_ref, spread_ref, states_ref, slope_a, slope_b, weight_a, weight_b, slope_ref,
    term_ref, guess_ref, adj_ref, part_ref, own_ref, other_ref,
):
    turn = pl.program_id(0)
    last = pl.num_programs(0) - 1
    rows, width = term_ref.shape
    part = spread_ref.shape[1] // 2

    def split(value):
        return halves(value, place_ref[2])

    def terms(scaled):
        product = lax.dot_general(
            states_ref[0], scaled, (((0,), (0,)), ((), ())), preferred_element_type=F32
        )
        part_ref[0] = product.astype(BF)

    @pl.when(turn == 0)
    def _():
        error = spread_ref[:, :part, :].reshape(rows, width).astype(F32)
        own_ref[...], other_ref[...] = split(term_ref[...].astype(F32) + error)

    @pl.when(turn < last)
    def _():
        scaled = (own_ref[...] * slope_a[0]).astype(BF)
        scaled_other = (other_ref[...] * slope_b[0]).astype(BF)
        terms(scaled)
        product = back_product(scaled, weight_a[0]) + back_product(scaled_other, weight_b[0])
        own, other = split(step_size * product)
        current = own_ref[...] + own
        own_ref[...] = current
        other_ref[...] += other
        adj_ref[0] = current.astype(BF)

    @pl.when(turn == last)
    def _():
        terms((own_ref[...] * split(slope_ref[0])[0]).astype(BF))
        error = spread_ref[:, part:, :].reshape(rows, width).astype(F32)
        adj_ref[0] = split(guess_ref[...].astype(F32) + error)[0].astype(BF)


def correct(place, spread, states, slopes_a, slopes_b, weights_a, weights_b, slope, terminal, guess):
    layers, rows, width = states.shape
    half = width // 2
    top = layers - 1
    lower = lambda t, place: (jnp.maximum(top - 1 - t, 0), 0, 0)
    whole = lambda v: pl.BlockSpec(v.shape, lambda t, place: (0,) * v.ndim)
    layer = lambda v: pl.BlockSpec((1,) + v.shape[1:], lower)
    return pl.pallas_call(
        correct_kernel,
        grid_spec=pltpu.PrefetchScalarGridSpec(
            num_scalar_prefetch=1,
            grid=(layers,),
            in_specs=[
                whole(spread),
                pl.BlockSpec((1, rows, width), lambda t, place: (top - t, 0, 0)),
                layer(slopes_a),
                layer(slopes_b),
                layer(weights_a),
                layer(weights_b),
                whole(slope),
                whole(terminal),
                whole(guess),
            ],
            out_specs=[
                pl.BlockSpec((1, rows, half), lambda t, place: (top - t, 0, 0)),
                pl.BlockSpec((1, width, half), lambda t, place: (top - t, 0, 0)),
            ],
            scratch_shapes=[pltpu.VMEM((rows, half), F32)] * 2,
        ),
        out_shape=[
            jax.ShapeDtypeStruct((layers, rows, half), BF),
            jax.ShapeDtypeStruct((layers, width, half), BF),
        ],
        compiler_params=params(56),
        name="correct",
    )(place, spread, states, slopes_a, slopes_b, weights_a, weights_b, slope, terminal, guess)


def put(buffer, value, *index):
    lead = len(index)
    start = tuple(index) + (0,) * (buffer.ndim - lead)
    return lax.dynamic_update_slice(buffer, value.reshape((1,) * lead + value.shape), start)


def ring_gather(piece, beside):
    count = lax.axis_size("dp")
    me = lax.axis_index("dp")
    rows = piece.shape[0]
    mid = rows // 2
    whole = put(jnp.zeros((count,) + piece.shape, piece.dtype), piece, me)
    up = down = piece
    for hop in range(1, count // 2):
        if hop == count // 2 - 1:
            up, down, beside = lax.optimization_barrier((up, down, beside))
        up, down = rotated(up, "dp", 1), rotated(down, "dp", -1)
        whole = put(whole, up, (me - hop) % count)
        whole = put(whole, down, (me + hop) % count)
    far = jnp.concatenate([rotated(up[:mid], "dp", 1), rotated(down[mid:], "dp", -1)], 0)
    whole = put(whole, far, (me + count // 2) % count)
    return whole.reshape((count * rows,) + piece.shape[1:]), beside


def body(states, weights, guess_points, cotangent):
    slabs = lax.axis_size(LAYER)
    slab = lax.axis_index(LAYER)
    half_index = lax.axis_index("mp")
    place = jnp.stack([lax.axis_index("x"), lax.axis_index("core"), half_index]).astype(jnp.int32)
    blocks = lax.axis_size(RING)
    layers, rows, width = states.shape
    mid = width // 2
    guess = guess_points[0]

    rest_own = lax.all_gather(weights[1:], "dp", axis=1, tiled=True)
    shard, far_shard = weights[0], swapped(weights[0], "mp")
    shard = jnp.where(
        half_index == 0,
        jnp.concatenate([shard, far_shard], -1),
        jnp.concatenate([far_shard, shard], -1),
    )
    coarse, rest_far = ring_gather(shard, swapped(weights[1:], "mp"))
    rest_other = lax.all_gather(rest_far, "dp", axis=1, tiled=True)
    next_guess = lax.ppermute(guess, LAYER, [(i, i - 1) for i in range(1, slabs)])
    terminal = jnp.where(slab == slabs - 1, cotangent, next_guess)
    slope = slopes_of(states, coarse[None], 0)

    ahead = rotated(coarse, "x", -1)
    behind = rotated(coarse, "x", 1)
    slopes_own = slopes_of(states, rest_own, 1)
    keep, send = half_step(place, (terminal,), states, None, rest_own, layers - 1)
    got = swapped(send, "mp")
    for layer in range(layers - 2, 0, -1):
        keep, send = half_step(place, (keep, got), states, slopes_own, rest_own, layer, layer == 1)
        got = swapped(send, "mp")
    pack = last_step(keep, got, slope, coarse, guess, blocks)
    ahead, behind, pack = lax.optimization_barrier((ahead, behind, pack))
    front, back = rotated(ahead[:mid], "x", -1), rotated(behind[mid:], "x", 1)
    pack = lax.all_to_all(pack, RING, 0, 0, tiled=True)
    front, back, pack = lax.optimization_barrier((front, back, pack))
    across = jnp.concatenate([front, back], 0)
    ring = (coarse, ahead, across, behind)
    ring = ring + tuple(swapped(value, "core") for value in ring)
    slopes_other = slopes_of(states, rest_other, 1)

    incoming = jnp.zeros((pack.shape[1] // 2, width), BF)
    stages = lax.axis_size("zl")
    for stage in range(stages):
        errors, lowest = chain(place, pack, ring, incoming)
        if stage < stages - 1:
            incoming = lax.ppermute(lowest, "zl", [(i, i - 1) for i in range(1, stages)])
    spread = lax.all_to_all(errors, RING, 0, 0, tiled=True)

    adjoint, partial = correct(
        place, spread, states, slopes_own, slopes_other, rest_own, rest_other, slope, terminal, guess
    )
    grads = lax.psum_scatter(partial, "dp", scatter_dimension=1, tiled=True)
    return adjoint, step_size * grads.astype(F32)


def solution(mesh):
    slabs, rows, halves = (mesh.shape[name] for name in ("layer", "dp", "mp"))
    fine = Mesh(
        mesh.devices.reshape(slabs // 8, 4, 2, rows, halves), ("zl", "x", "core", "dp", "mp")
    )
    return jax.shard_map(
        body,
        mesh=fine,
        in_specs=(
            P(LAYER, "dp", None),
            P(LAYER, "dp", "mp"),
            P(LAYER, "dp", None),
            P("dp", None),
        ),
        out_specs=(P(LAYER, "dp", "mp"), P(LAYER, "dp", "mp")),
        check_vma=False,
    )
```

```python
import functools

import jax
import jax.numpy as jnp
from jax import lax
from jax.experimental import pallas as pl
from jax.experimental.pallas import tpu as pltpu
from jax.sharding import Mesh
from jax.sharding import PartitionSpec as P

step_size = 0.1
BF = jnp.bfloat16
F32 = jnp.float32
LAYER = ("zl", "x", "core")
RING = ("x", "core")


def back_product(scaled, weight):
    return lax.dot_general(scaled, weight, (((1,), (1,)), ((), ())), preferred_element_type=F32)


def swapped(value, axis):
    return lax.ppermute(value, axis, [(0, 1), (1, 0)])


def rotated(value, axis, steps):
    count = lax.axis_size(axis)
    return lax.ppermute(value, axis, [(i, (i + steps) % count) for i in range(count)])


def halves(value, index):
    half = value.shape[1] // 2
    low, high = value[:, :half], value[:, half:]
    return jnp.where(index == 0, low, high), jnp.where(index == 0, high, low)


def params(mib):
    return pltpu.CompilerParams(vmem_limit_bytes=mib * 2**20)


def cost(flops, moved):
    return pl.CostEstimate(flops=flops, bytes_accessed=moved, transcendentals=0)


def relax_kernel(
    blocks, place_ref, states_ref, own_ref, far_ref, far_low_ref, term_ref, guess_ref,
    slope_own, slope_far, pack_ref, v_own, v_far,
):
    turn = pl.program_id(0)
    last = pl.num_programs(0) - 1
    rows, width = term_ref.shape

    @pl.when(turn == 0)
    def _():
        v_own[...], v_far[...] = halves(term_ref[...].astype(F32), place_ref[2])

    def part(weight, slope_ref, v_ref):
        tangent = jnp.tanh(jnp.dot(states_ref[0], weight, preferred_element_type=F32))
        slope = 1.0 - tangent * tangent
        slope_ref[0] = slope
        scaled = (v_ref[...] * slope).astype(BF)
        return slope, back_product(scaled, weight)

    def step(far):
        slope, product = part(own_ref[0], slope_own, v_own)
        slope_other, product_other = part(far, slope_far, v_far)
        own, other = halves(step_size * (product + product_other), place_ref[2])
        v_own[...] += own
        v_far[...] += other
        return slope, slope_other

    def joined(own, far):
        first = place_ref[2] == 0
        return jnp.concatenate([jnp.where(first, own, far), jnp.where(first, far, own)], 1)

    @pl.when(turn < last)
    def _():
        step(far_ref[0])

    @pl.when(turn == last)
    def _():
        slope = joined(*step(far_low_ref[...]))
        residual = joined(v_own[...], v_far[...]) - guess_ref[...].astype(F32)
        size = rows // blocks
        pack_ref[:, :size, :] = residual.astype(BF).reshape(blocks, size, width)
        pack_ref[:, size:, :] = slope.astype(BF).reshape(blocks, size, width)


def relax(place, states, own, far, far_low, terminal, guess, blocks):
    layers, rows, width = states.shape
    half = width // 2
    top = layers - 1
    layer = lambda t, place: (top - t, 0, 0)
    whole = lambda v: pl.BlockSpec(v.shape, lambda t, place: (0,) * v.ndim)
    pack = jax.ShapeDtypeStruct((blocks, 2 * rows // blocks, width), BF)
    slopes = jax.ShapeDtypeStruct((layers, rows, half), F32)
    return pl.pallas_call(
        functools.partial(relax_kernel, blocks),
        grid_spec=pltpu.PrefetchScalarGridSpec(
            num_scalar_prefetch=1,
            grid=(layers,),
            in_specs=[
                pl.BlockSpec((1, rows, width), layer),
                pl.BlockSpec((1, width, half), layer),
                pl.BlockSpec((1, width, half), lambda t, place: (jnp.maximum(top - 1 - t, 0), 0, 0)),
                whole(far_low),
                whole(terminal),
                whole(guess),
            ],
            out_specs=[
                pl.BlockSpec((1, rows, half), layer),
                pl.BlockSpec((1, rows, half), layer),
                whole(pack),
            ],
            scratch_shapes=[pltpu.VMEM((rows, half), F32)] * 2,
        ),
        out_shape=[slopes, slopes, pack],
        compiler_params=params(56),
        cost_estimate=cost(4 * layers * rows * width * width, 2 * layers * width * width),
        name="relax",
    )(place, states, own, far, far_low, terminal, guess)


def chain_kernel(chips, place_ref, pack_ref, in_ref, *rest):
    mine, other, (out_ref, low_ref, held, arrived) = rest[:5], rest[5:10], rest[10:]
    count = 2 * chips
    part = in_ref.shape[0]
    scale = 4 * step_size

    def fetch(source, point, side):
        return pltpu.make_async_copy(source, held.at[point, side], arrived.at[point, side])

    def source_of(group, hop, side):
        here, ahead, behind, front, back = group
        if hop == 2:
            return (front, back)[side]
        return (here, ahead, None, behind)[hop].at[side]

    for point in range(count - 1, -1, -1):
        distance = lax.rem(point // 2 - place_ref[0] + chips, chips)
        same = place_ref[1] == point % 2
        for hop in range(chips):
            @pl.when((distance == hop) & same)
            def _():
                for side in range(2):
                    fetch(source_of(mine, hop, side), point, side).start()

            @pl.when((distance == hop) & jnp.logical_not(same))
            def _():
                for side in range(2):
                    fetch(source_of(other, hop, side), point, side).start()

    short = in_ref[...]
    for point in range(count - 1, -1, -1):
        v = short.astype(F32)
        scaled = (v * pack_ref[point, part:, :].astype(F32)).astype(BF)
        out_ref[point, :part, :] = short
        base = v + pack_ref[point, :part, :].astype(F32)
        own, far = halves(scaled, place_ref[2])
        fetch(mine[3], point, 0).wait()
        product = back_product(own, held[point, 0])
        fetch(mine[3], point, 1).wait()
        product += back_product(far, held[point, 1])
        short = (base + scale * product).astype(BF)
        out_ref[point, part:, :] = short
    low_ref[...] = short


def chain(place, pack, sources, incoming):
    chips = lax.axis_size("x")
    weight = sources[0].shape
    whole = lambda v: pl.BlockSpec(v.shape, lambda t, place: (0,) * v.ndim)
    return pl.pallas_call(
        functools.partial(chain_kernel, chips),
        grid_spec=pltpu.PrefetchScalarGridSpec(
            num_scalar_prefetch=1,
            grid=(1,),
            in_specs=[whole(pack), whole(incoming)]
            + [pl.BlockSpec(memory_space=pl.ANY)] * len(sources),
            out_specs=[whole(pack), whole(incoming)],
            scratch_shapes=[
                pltpu.VMEM((2 * chips,) + weight, BF),
                pltpu.SemaphoreType.DMA((2 * chips, 2)),
            ],
        ),
        out_shape=[
            jax.ShapeDtypeStruct(pack.shape, BF),
            jax.ShapeDtypeStruct(incoming.shape, BF),
        ],
        compiler_params=params(40),
        cost_estimate=cost(2 * pack.size * weight[1], 8 * chips * weight[1] ** 2),
        name="chain",
    )(place, pack, incoming, *sources)


def correct_kernel(
    place_ref, spread_ref, states_ref, slope_a, slope_b, weight_a, weight_b,
    term_ref, guess_ref, adj_ref, part_ref, own_ref, other_ref,
):
    turn = pl.program_id(0)
    last = pl.num_programs(0) - 1
    rows, width = term_ref.shape
    part = spread_ref.shape[1] // 2

    def split(value):
        return halves(value, place_ref[2])

    def terms(scaled):
        product = lax.dot_general(
            states_ref[0], scaled, (((0,), (0,)), ((), ())), preferred_element_type=F32
        )
        part_ref[0] = product.astype(BF)

    @pl.when(turn == 0)
    def _():
        error = spread_ref[:, :part, :].reshape(rows, width).astype(F32)
        own_ref[...], other_ref[...] = split(term_ref[...].astype(F32) + error)

    @pl.when(turn < last)
    def _():
        scaled = (own_ref[...] * slope_a[0]).astype(BF)
        scaled_other = (other_ref[...] * slope_b[0]).astype(BF)
        terms(scaled)
        product = back_product(scaled, weight_a[0]) + back_product(scaled_other, weight_b[0])
        own, other = split(step_size * product)
        current = own_ref[...] + own
        own_ref[...] = current
        other_ref[...] += other
        adj_ref[0] = current.astype(BF)

    @pl.when(turn == last)
    def _():
        terms((own_ref[...] * slope_a[0]).astype(BF))
        error = spread_ref[:, part:, :].reshape(rows, width).astype(F32)
        adj_ref[0] = split(guess_ref[...].astype(F32) + error)[0].astype(BF)


def correct(place, spread, states, slopes_a, slopes_b, weights_a, weights_b, terminal, guess):
    layers, rows, width = states.shape
    half = width // 2
    top = layers - 1
    lower = lambda t, place: (jnp.maximum(top - 1 - t, 0), 0, 0)
    whole = lambda v: pl.BlockSpec(v.shape, lambda t, place: (0,) * v.ndim)
    layer = lambda v: pl.BlockSpec((1,) + v.shape[1:], lambda t, place: (top - t, 0, 0))
    return pl.pallas_call(
        correct_kernel,
        grid_spec=pltpu.PrefetchScalarGridSpec(
            num_scalar_prefetch=1,
            grid=(layers,),
            in_specs=[
                whole(spread),
                pl.BlockSpec((1, rows, width), lambda t, place: (top - t, 0, 0)),
                layer(slopes_a),
                layer(slopes_b),
                layer(weights_a),
                pl.BlockSpec((1, width, half), lower),
                whole(terminal),
                whole(guess),
            ],
            out_specs=[
                pl.BlockSpec((1, rows, half), lambda t, place: (top - t, 0, 0)),
                pl.BlockSpec((1, width, half), lambda t, place: (top - t, 0, 0)),
            ],
            scratch_shapes=[pltpu.VMEM((rows, half), F32)] * 2,
        ),
        out_shape=[
            jax.ShapeDtypeStruct((layers, rows, half), BF),
            jax.ShapeDtypeStruct((layers, width, half), BF),
        ],
        compiler_params=params(56),
        name="correct",
    )(place, spread, states, slopes_a, slopes_b, weights_a, weights_b, terminal, guess)


def put(buffer, value, *index):
    lead = len(index)
    start = tuple(index) + (0,) * (buffer.ndim - lead)
    return lax.dynamic_update_slice(buffer, value.reshape((1,) * lead + value.shape), start)


def ring_gather(piece, beside):
    count = lax.axis_size("dp")
    me = lax.axis_index("dp")
    rows = piece.shape[0]
    mid = rows // 2
    whole = put(jnp.zeros((count,) + piece.shape, piece.dtype), piece, me)
    up = down = piece
    for hop in range(1, count // 2):
        if hop == count // 2 - 1:
            up, down, beside = lax.optimization_barrier((up, down, beside))
        up, down = rotated(up, "dp", 1), rotated(down, "dp", -1)
        whole = put(whole, up, (me - hop) % count)
        whole = put(whole, down, (me + hop) % count)
    far = jnp.concatenate([rotated(up[:mid], "dp", 1), rotated(down[mid:], "dp", -1)], 0)
    whole = put(whole, far, (me + count // 2) % count)
    return whole.reshape((count * rows,) + piece.shape[1:]), beside


def body(states, weights, guess_points, cotangent):
    slabs = lax.axis_size(LAYER)
    slab = lax.axis_index(LAYER)
    half_index = lax.axis_index("mp")
    place = jnp.stack([lax.axis_index("x"), lax.axis_index("core"), half_index]).astype(jnp.int32)
    blocks = lax.axis_size(RING)
    layers, rows, width = states.shape
    guess = guess_points[0]

    own = lax.all_gather(weights, "dp", axis=1, tiled=True)
    next_guess = lax.ppermute(guess, LAYER, [(i, i - 1) for i in range(1, slabs)])
    far_low, (shards, next_guess) = ring_gather(
        swapped(weights[0], "mp"), (swapped(weights[1:], "mp"), next_guess)
    )
    far = lax.all_gather(shards, "dp", axis=1, tiled=True)
    terminal = jnp.where(slab == slabs - 1, cotangent, next_guess)

    here = jnp.stack([own[0], far_low])
    ahead = rotated(here, "x", -1)
    behind = rotated(here, "x", 1)
    front, back = rotated(ahead[0], "x", -1), rotated(behind[1], "x", 1)

    slopes_own, slopes_far, pack = relax(
        place, states, own, far, far_low, terminal, guess, blocks
    )
    pack = lax.all_to_all(pack, RING, 0, 0, tiled=True)
    front, back, pack = lax.optimization_barrier((front, back, pack))
    ring = (here, ahead, behind, front, back)
    ring = ring + tuple(swapped(value, "core") for value in ring)

    incoming = jnp.zeros((pack.shape[1] // 2, width), BF)
    stages = lax.axis_size("zl")
    for stage in range(stages):
        errors, lowest = chain(place, pack, ring, incoming)
        if stage < stages - 1:
            incoming = lax.ppermute(lowest, "zl", [(i, i - 1) for i in range(1, stages)])
    spread = lax.all_to_all(errors, RING, 0, 0, tiled=True)

    adjoint, partial = correct(
        place, spread, states, slopes_own, slopes_far, own, far, terminal, guess
    )
    grads = lax.psum_scatter(partial, "dp", scatter_dimension=1, tiled=True)
    return adjoint, step_size * grads.astype(F32)


def solution(mesh):
    slabs, rows, halves = (mesh.shape[name] for name in ("layer", "dp", "mp"))
    fine = Mesh(
        mesh.devices.reshape(slabs // 8, 4, 2, rows, halves), ("zl", "x", "core", "dp", "mp")
    )
    return jax.shard_map(
        body,
        mesh=fine,
        in_specs=(
            P(LAYER, "dp", None),
            P(LAYER, "dp", "mp"),
            P(LAYER, "dp", None),
            P("dp", None),
        ),
        out_specs=(P(LAYER, "dp", "mp"), P(LAYER, "dp", "mp")),
        check_vma=False,
    )
```
